32 devices in a mesh: groups: 2 (over y), context: 16 (over z, x, core).
Axes of the slice: x: 2, y: 2, z: 4, core: 2. Of those that a mesh axis runs over, the one named last changes fastest.
Arguments:
- queries: bfloat16 [8192, 8192], P(('groups', 'context')), parts along dimension 0, may hold values from -68 to 68
- keys: bfloat16 [8192, 1024], P(('groups', 'context')), parts along dimension 0, may hold values from -6 to 6
- values: bfloat16 [8192, 1024], P(('groups', 'context')), parts along dimension 0, may hold values from -6 to 6
- segments: int32 [8192], P(('groups', 'context')), parts along dimension 0, may hold values from 0 to 9, never falling along the last dimension, each value on 1 to 768 neighbouring positions
Outputs:
- rotated: bfloat16 [8192, 8192], P(('groups', 'context')), parts along dimension 0
The draws below stay inside these ranges and needn't reach their ends.
There are 2 independent parts, one for each index of `groups`. The reference program is written for one: setup_inputs(seed, part) draws one part's arguments, and reference() takes and returns one part's arrays. A program takes and returns all parts, laid end to end along the dimension named above; each array names one. Nothing has to cross between parts.
Inputs may be any that keep to these rules, and one draw needn't show every extreme that they name: `segments`: document numbers never fall along the block; each document holds 1 to 768 tokens and one holds exactly 768.
All inputs are finite; a program needn't handle non-finite values.
Results may differ from the reference program's by a relative error of at most 0.0054.
Values may be sent and summed in bfloat16 or wider, within the bound.
A program may use at most 64 MiB of HBM per device.

```python
import math
import jax
import jax.numpy as jnp
import numpy as np
from jax import lax

HEADS = 64
KVH = 8
HD = 128
TOK_DEV = 256
PRIOR = 3
MOST = 768
STRETCH = 4096
DOCS = 10
N_CONTEXT = 16


def draw_queries(key, part):
    shape = (STRETCH, HEADS * HD)
    base = jnp.clip(jax.random.normal(key, shape, jnp.float32), -6.0, 6.0)
    return base.astype(jnp.bfloat16)


def block_levels(stream_key, dims, shards, least, largest):
    def one(dim, parts):
        draws = jax.random.uniform(jax.random.fold_in(jax.random.fold_in(stream_key, 6), dim), (parts,), jnp.float32, least / len(shards), largest / len(shards))
        return jnp.repeat(jnp.exp(draws), dims[dim] // parts).reshape((-1,) + (1,) * (len(dims) - dim - 1))

    level = one(*shards[0])
    for cut in shards[1:]:
        level = level * one(*cut)
    return level


def length_profile(number_of, total, bound, lean):
    weights = [(1 << 20) // math.isqrt(standing ** lean) + 1 for standing in range(2, number_of + 1)]
    spare, counts = total - bound - (number_of - 1), [1] * (number_of - 1)
    while spare > 0:
        candidates = [i for i in range(number_of - 1) if counts[i] < bound]
        pool, remaining = sum([weights[i] for i in candidates]), spare
        for i in candidates:
            addition = min(bound - counts[i], max(1, remaining * weights[i] // pool), spare)
            counts[i] = counts[i] + addition
            spare = spare - addition
    return np.array([bound] + counts)


def uneven_parts(stream_key, amount, total, reach, lean):
    if amount == 2:
        one = jax.random.randint(stream_key, (), max(1, total - reach), min(reach, total - 1) + 1)
        return jnp.stack([one, total - one])
    sizes = jnp.asarray(length_profile(amount, total, reach, lean), jnp.int32)
    couples = (amount - 1) // 2
    source_of, receiver = sizes[1:1 + 2 * couples:2], sizes[2:2 + 2 * couples:2]
    margin = jnp.minimum(source_of - 1, reach - receiver)
    passed = jax.random.randint(jax.random.fold_in(stream_key, 1), (couples,), 0, 1 << 20) % (margin + 1)
    sizes = sizes.at[1:1 + 2 * couples:2].set(source_of - passed).at[2:2 + 2 * couples:2].set(receiver + passed)
    return sizes[jax.random.permutation(jax.random.fold_in(stream_key, 2), amount)]


def normal_values(stream_key, dims, scale, most, shards=(), kind=jnp.bfloat16):
    loudness = block_levels(stream_key, dims, shards, -0.22, 0.18) if shards else 1.0
    array = jax.random.normal(stream_key, dims, jnp.float32) * scale * loudness
    return jnp.minimum(jnp.maximum(array, -most), most).astype(kind)


def setup_inputs(seed: int = 0, part: int = 0) -> dict:
    arg_keys = jax.random.split(jax.random.key(seed), 5)
    part_keys = jax.random.split(jax.random.fold_in(arg_keys[4], part), 5)
    return {
        "queries": draw_queries(jax.random.fold_in(jax.random.fold_in(arg_keys[4], part), 71), part),
        "keys": normal_values(part_keys[1], (STRETCH, KVH * HD), 1.0, 6.0, ((0, 16),)),
        "values": normal_values(part_keys[2], (STRETCH, KVH * HD), 1.0, 6.0, ((0, 16),)),
        "segments": jnp.searchsorted(jnp.cumsum(uneven_parts(part_keys[3], DOCS, STRETCH, MOST, 0)), jnp.arange(STRETCH), side="right").astype(jnp.int32),
    }


def build_mixer():
    rows = jnp.arange(HEADS, dtype=jnp.int32)[:, None]
    cols = jnp.arange(HEADS, dtype=jnp.int32)[None, :]
    both = jnp.bitwise_and(rows, cols)
    parity = jnp.zeros((HEADS, HEADS), jnp.int32)
    for level in range(HEADS.bit_length()):
        parity = parity + jnp.bitwise_and(jnp.right_shift(both, level), 1)
    signs = 1.0 - 2.0 * jnp.bitwise_and(parity, 1).astype(jnp.float32)
    return (signs / jnp.sqrt(jnp.float32(HEADS))).astype(jnp.bfloat16)

def attend(query_rows, seg_rows, key_rows, value_rows, seg_keys, offset):
    count = query_rows.shape[0]
    length = key_rows.shape[0]
    group = HEADS // KVH
    query_idx = jnp.arange(count, dtype=jnp.int32)[:, None] + offset
    key_idx = jnp.arange(length, dtype=jnp.int32)[None, :]
    allowed = (seg_keys[None, :] == seg_rows[:, None]) & (key_idx <= query_idx)
    query_heads = jnp.transpose(query_rows.reshape(count, KVH, group, HD), (1, 0, 2, 3))
    key_heads = jnp.transpose(key_rows.reshape(length, KVH, HD), (1, 0, 2))
    value_heads = jnp.transpose(value_rows.reshape(length, KVH, HD), (1, 0, 2))

    def one_head(items):
        qh, kh, vh = items
        scores = jnp.einsum('tqd,ld->qtl', qh.astype(jnp.float32), kh.astype(jnp.float32)) / jnp.sqrt(jnp.float32(HD))
        masked = jnp.where(allowed[None], scores, -jnp.inf)
        top = lax.optimization_barrier(jnp.max(masked, axis=-1, keepdims=True))
        weights = jnp.where(allowed[None], jnp.exp(scores - top), 0.0)
        total = lax.optimization_barrier(jnp.sum(weights, axis=-1, keepdims=True))
        probs = weights.astype(jnp.bfloat16)
        summed = jnp.einsum('qtl,ld->tqd', probs.astype(jnp.float32), vh.astype(jnp.float32))
        return summed / jnp.transpose(total, (1, 0, 2))
    outs = lax.map(one_head, (query_heads, key_heads, value_heads))
    attended = jnp.transpose(outs, (1, 0, 2, 3)).reshape(count, HEADS, HD).astype(jnp.bfloat16)
    mixed = jnp.einsum('hk,tkd->thd', build_mixer().astype(jnp.float32), attended.astype(jnp.float32))
    return mixed.astype(jnp.bfloat16).reshape(count, HEADS * HD)

def reference(queries, keys, values, segments):
    seg_plus = segments + 1
    front = PRIOR * TOK_DEV
    keys_pad = jnp.concatenate([jnp.zeros((front, KVH * HD), jnp.bfloat16), keys], 0)
    values_pad = jnp.concatenate([jnp.zeros((front, KVH * HD), jnp.bfloat16), values], 0)
    seg_pad = jnp.concatenate([jnp.zeros((front,), jnp.int32), seg_plus], 0)
    span = (PRIOR + 1) * TOK_DEV

    def block(index):
        start = (index * TOK_DEV).astype(jnp.int32)
        query_rows = lax.dynamic_slice_in_dim(queries, start, TOK_DEV, 0)
        seg_rows = lax.dynamic_slice_in_dim(seg_plus, start, TOK_DEV, 0)
        key_rows = lax.dynamic_slice_in_dim(keys_pad, start, span, 0)
        value_rows = lax.dynamic_slice_in_dim(values_pad, start, span, 0)
        seg_keys = lax.dynamic_slice_in_dim(seg_pad, start, span, 0)
        return attend(query_rows, seg_rows, key_rows, value_rows, seg_keys, front)
    blocks = lax.map(block, jnp.arange(N_CONTEXT, dtype=jnp.int32))
    return blocks.reshape(STRETCH, HEADS * HD)
```

```python
import functools
import math

import jax
import jax.numpy as jnp
from jax import lax
from jax.experimental import pallas as pl
from jax.experimental.pallas import tpu as pltpu
from jax.sharding import PartitionSpec as P

HEADS = 64
KVH = 8
HD = 128
PRIOR = 3
GROUP = HEADS // KVH
AXIS = "context"
LOW = -1e30
SCALE = math.log2(math.e) / math.sqrt(HD)


def butterfly(parts):
    parts = list(parts)
    step = 1
    while step < len(parts):
        for a in range(len(parts)):
            if a & step == 0:
                low, high = parts[a], parts[a + step]
                parts[a], parts[a + step] = low + high, low - high
        step *= 2
    return parts


def attend_kernel(n, tok, q_hbm, k_hbm, v_hbm, seg_hbm, acc, qv, kv, segw, bias, q_sem, kv_sem, seg_sem, send_sem, recv_sem, seg_send, seg_recv):
    me = lax.axis_index(AXIS)
    pos = lax.rem(me, 4)
    odd = lax.rem(me, 2)
    partner = me + 1 - 2 * odd
    own = pl.ds(PRIOR * tok, tok)

    def slot(d):
        return pl.ds((PRIOR - d) * tok, tok)

    def local_kv(h):
        cols = pl.ds(h * HD, HD)
        return (
            pltpu.make_async_copy(k_hbm.at[:, cols], kv.at[h, 0, own, :], kv_sem.at[0, h]),
            pltpu.make_async_copy(v_hbm.at[:, cols], kv.at[h, 1, own, :], kv_sem.at[1, h]),
        )

    def local_q(g):
        cols = pl.ds(g * GROUP * HD, GROUP * HD)
        return pltpu.make_async_copy(q_hbm.at[:, cols], qv.at[:, cols], q_sem.at[g])

    local_seg = pltpu.make_async_copy(seg_hbm, segw.at[PRIOR], seg_sem)
    local_seg.start()
    for h in range(KVH):
        for copy in local_kv(h):
            copy.start()
    for g in range(KVH):
        local_q(g).start()

    barrier = pltpu.get_barrier_semaphore()
    for d in range(1, PRIOR + 1):
        for near in (me - d, me + d):
            @pl.when((near >= 0) & (near < n))
            def _():
                pl.semaphore_signal(barrier, inc=1, device_id={AXIS: near}, device_id_type=pl.DeviceIdType.MESH)

    for d in range(1, PRIOR + 1):
        @pl.when(me < d)
        def _():
            kv[:, :, slot(d), :] = jnp.zeros((KVH, 2, tok, HD), jnp.bfloat16)
            segw[PRIOR - d] = jnp.full((1, tok), -1, jnp.int32)

    pl.semaphore_wait(barrier, jnp.minimum(me, PRIOR) + jnp.minimum(n - 1 - me, PRIOR))

    def push(h, source, target, flow, to):
        return pltpu.make_async_remote_copy(
            src_ref=kv.at[h, :, source, :],
            dst_ref=kv.at[h, :, slot(target), :],
            send_sem=send_sem.at[flow],
            recv_sem=recv_sem.at[target - 1, h],
            device_id={AXIS: to},
            device_id_type=pl.DeviceIdType.MESH,
        )

    def seg_push(d):
        return pltpu.make_async_remote_copy(
            src_ref=segw.at[PRIOR],
            dst_ref=segw.at[PRIOR - d],
            send_sem=seg_send.at[d - 1],
            recv_sem=seg_recv.at[d - 1],
            device_id={AXIS: me + d},
            device_id_type=pl.DeviceIdType.MESH,
        )

    own_far = ((pos != 3) & (me + 2 < n), (odd == 1) & (me + 3 < n), odd == 0)

    def send_own(h):
        for d, flow, when in ((2, 0, own_far[0]), (3, 1, own_far[1]), (1, 2, own_far[2])):
            @pl.when(when)
            def _():
                push(h, own, d, flow, me + d).start()

    def wait_arrival(h, d):
        push(h, own, d, 0, partner).wait_recv()

    has = tuple(me >= d for d in range(1, PRIOR + 1))
    relays = (pos == 2) & has[2]

    def stage_a(h):
        @pl.when(relays)
        def _():
            wait_arrival(h, 3)
            push(h, slot(3), 2, 1, me - 1).start()

    def stage_b(h):
        @pl.when(has[1])
        def _():
            wait_arrival(h, 2)

            @pl.when(odd == 0)
            def _():
                push(h, slot(2), 3, 3, partner).start()

            @pl.when(odd == 1)
            def _():
                push(h, slot(2), 1, 3, partner).start()

    def stage_c(h):
        @pl.when(has[0])
        def _():
            wait_arrival(h, 1)

        @pl.when(has[2] & (pos != 2))
        def _():
            wait_arrival(h, 3)

    local_seg.wait()
    for d in range(1, PRIOR + 1):
        @pl.when(me + d < n)
        def _():
            seg_push(d).start()

    def start_own(h, carry):
        for copy in local_kv(h):
            copy.wait()
        send_own(h)
        return carry

    lax.fori_loop(0, KVH, start_own, 0)

    for d in range(1, PRIOR + 1):
        @pl.when(me >= d)
        def _():
            seg_push(d).wait_recv()

    seg_q = jnp.transpose(jnp.broadcast_to(segw[PRIOR], (128, tok)))
    for block in range((PRIOR + 1) * tok // 128):
        shard, part = divmod(block * 128, tok)
        seg_k = jnp.broadcast_to(segw[shard][:, part:part + 128], (tok, 128))
        key_idx = lax.broadcasted_iota(jnp.int32, (tok, 128), 1) + block * 128
        query_idx = lax.broadcasted_iota(jnp.int32, (tok, 128), 0) + PRIOR * tok
        allowed = (seg_k == seg_q) & (key_idx <= query_idx)
        bias[:, block * 128:(block + 1) * 128] = jnp.where(allowed, 0.0, LOW)

    half = tok // 2
    span = PRIOR * tok + half

    def one_group(g):
        ones = jnp.ones((span, HD), jnp.bfloat16)
        done = []
        for j in range(GROUP):
            pieces = []
            for rb in range(2):
                rows = pl.ds(rb * half, half)
                keys = pl.ds(rb * half, span)
                q = qv[rows, pl.ds(pl.multiple_of((g * GROUP + j) * HD, HD), HD)]
                s = lax.dot_general(q, kv[g, 0, keys, :], (((1,), (1,)), ((), ())), preferred_element_type=jnp.float32)
                s = s + bias[rows, keys]
                top = jnp.max(s, axis=-1, keepdims=True)
                p = jnp.exp2((s - top) * SCALE).astype(jnp.bfloat16)
                wide = jnp.concatenate([kv[g, 1, keys, :], ones], axis=1)
                o = jnp.dot(p, wide, preferred_element_type=jnp.float32)
                pieces.append((o[:, :HD] / o[:, HD:]).astype(jnp.bfloat16).astype(jnp.float32))
            done.append(pieces)
        for rb in range(2):
            mixed = butterfly([done[j][rb] for j in range(GROUP)])
            for j in range(GROUP):
                acc[g, j, pl.ds(rb * half, half), :] = mixed[j]

    stage_a(0)
    stage_a(1)
    stage_b(0)

    def step(g, carry):
        @pl.when(g + 2 < KVH)
        def _():
            stage_a(g + 2)

        @pl.when(g + 1 < KVH)
        def _():
            stage_b(g + 1)

        stage_c(g)
        local_q(g).wait()
        one_group(g)
        return carry

    lax.fori_loop(0, KVH, step, 0)

    def drain(flow):
        pltpu.make_async_remote_copy(
            src_ref=kv.at[:, :, own, :],
            dst_ref=kv.at[:, :, own, :],
            send_sem=send_sem.at[flow],
            recv_sem=recv_sem.at[0, 0],
            device_id={AXIS: partner},
            device_id_type=pl.DeviceIdType.MESH,
        ).wait_send()

    for flow, when in enumerate((own_far[0], own_far[1] | relays, own_far[2], has[1])):
        @pl.when(when)
        def _():
            drain(flow)

    for d in range(1, PRIOR + 1):
        @pl.when(me + d < n)
        def _():
            seg_push(d).wait_send()


def mix_kernel(rows, acc, out):
    start = pl.multiple_of(pl.program_id(0) * rows, rows)
    for j in range(GROUP):
        mixed = butterfly([acc[g, j, pl.ds(start, rows), :] for g in range(KVH)])
        for g in range(KVH):
            col = (g * GROUP + j) * HD
            out[:, col:col + HD] = (mixed[g] * (1.0 / math.sqrt(HEADS))).astype(jnp.bfloat16)


def per_device(n, queries, keys, values, segments):
    tok = queries.shape[0]
    hbm = pl.BlockSpec(memory_space=pl.ANY)
    vmem = pl.BlockSpec(memory_space=pltpu.VMEM)
    acc = pl.pallas_call(
        functools.partial(attend_kernel, n, tok),
        out_shape=pltpu.VMEM((KVH, GROUP, tok, HD), jnp.float32),
        in_specs=[hbm] * 4,
        out_specs=vmem,
        scratch_shapes=[
            pltpu.VMEM((tok, HEADS * HD), jnp.bfloat16),
            pltpu.VMEM((KVH, 2, (PRIOR + 1) * tok, HD), jnp.bfloat16),
            pltpu.VMEM((PRIOR + 1, 1, tok), jnp.int32),
            pltpu.VMEM((tok, (PRIOR + 1) * tok), jnp.float32),
            pltpu.SemaphoreType.DMA((KVH,)),
            pltpu.SemaphoreType.DMA((2, KVH)),
            pltpu.SemaphoreType.DMA,
            pltpu.SemaphoreType.DMA((4,)),
            pltpu.SemaphoreType.DMA((PRIOR, KVH)),
            pltpu.SemaphoreType.DMA((PRIOR,)),
            pltpu.SemaphoreType.DMA((PRIOR,)),
        ],
        compiler_params=pltpu.CompilerParams(
            collective_id=0, has_side_effects=True, vmem_limit_bytes=50 * 2**20
        ),
        name="attend",
    )(queries, keys, values, segments.reshape(1, tok))
    rows = 32
    return pl.pallas_call(
        functools.partial(mix_kernel, rows),
        grid=(tok // rows,),
        out_shape=jax.ShapeDtypeStruct((tok, HEADS * HD), jnp.bfloat16),
        in_specs=[vmem],
        out_specs=pl.BlockSpec((rows, HEADS * HD), lambda i: (i, 0)),
        compiler_params=pltpu.CompilerParams(vmem_limit_bytes=16 * 2**20),
        name="mix",
    )(acc)


def solution(mesh):
    spec = P(("groups", AXIS), None)
    return jax.shard_map(
        functools.partial(per_device, mesh.shape[AXIS]),
        mesh=mesh,
        in_specs=(spec, spec, spec, P(("groups", AXIS))),
        out_specs=spec,
        check_vma=False,
    )
```

```python
import functools
import math

import jax
import jax.numpy as jnp
from jax import lax
from jax.experimental import pallas as pl
from jax.experimental.pallas import tpu as pltpu
from jax.sharding import PartitionSpec as P

HEADS = 64
KVH = 8
HD = 128
PRIOR = 3
GROUP = HEADS // KVH
AXIS = "context"
LOW = -1e30
BATCH = 8
CHUNKS = 2 * KVH
AHEAD = 3
SCALE = math.log2(math.e) / math.sqrt(HD)


def butterfly(parts):
    parts = list(parts)
    step = 1
    while step < len(parts):
        for a in range(len(parts)):
            if a & step == 0:
                low, high = parts[a], parts[a + step]
                parts[a], parts[a + step] = low + high, low - high
        step *= 2
    return parts


def attend_kernel(n, tok, q_hbm, k_hbm, v_hbm, seg_hbm, acc, qv, kv, segw, bias, q_sem, kv_sem, seg_sem, send_sem, recv_sem, seg_send, seg_recv):
    me = lax.axis_index(AXIS)
    pos = lax.rem(me, 4)
    odd = lax.rem(me, 2)
    partner = me + 1 - 2 * odd
    own = pl.ds(PRIOR * tok, tok)

    def slot(d):
        return pl.ds((PRIOR - d) * tok, tok)

    def local_kv(h):
        cols = pl.ds(h * HD, HD)
        return (
            pltpu.make_async_copy(k_hbm.at[:, cols], kv.at[2 * h, own, :], kv_sem.at[2 * h]),
            pltpu.make_async_copy(v_hbm.at[:, cols], kv.at[2 * h + 1, own, :], kv_sem.at[2 * h + 1]),
        )

    def local_q(g):
        cols = pl.ds(g * GROUP * HD, GROUP * HD)
        return pltpu.make_async_copy(q_hbm.at[:, cols], qv.at[:, cols], q_sem.at[g])

    local_seg = pltpu.make_async_copy(seg_hbm, segw.at[PRIOR], seg_sem)
    local_seg.start()
    for h in range(KVH):
        for copy in local_kv(h):
            copy.start()
    for g in range(KVH):
        local_q(g).start()

    barrier = pltpu.get_barrier_semaphore()
    for d in range(1, PRIOR + 1):
        for near in (me - d, me + d):
            @pl.when((near >= 0) & (near < n))
            def _():
                pl.semaphore_signal(barrier, inc=1, device_id={AXIS: near}, device_id_type=pl.DeviceIdType.MESH)

    for d in range(1, PRIOR + 1):
        @pl.when(me < d)
        def _():
            kv[:, slot(d), :] = jnp.zeros((CHUNKS, tok, HD), jnp.bfloat16)
            segw[PRIOR - d] = jnp.full((1, tok), -1, jnp.int32)

    pl.semaphore_wait(barrier, jnp.minimum(me, PRIOR) + jnp.minimum(n - 1 - me, PRIOR))

    def push(h, source, target, flow, to):
        return pltpu.make_async_remote_copy(
            src_ref=kv.at[h, source, :],
            dst_ref=kv.at[h, slot(target), :],
            send_sem=send_sem.at[flow],
            recv_sem=recv_sem.at[target - 1, h],
            device_id={AXIS: to},
            device_id_type=pl.DeviceIdType.MESH,
        )

    def seg_push(d):
        return pltpu.make_async_remote_copy(
            src_ref=segw.at[PRIOR],
            dst_ref=segw.at[PRIOR - d],
            send_sem=seg_send.at[d - 1],
            recv_sem=seg_recv.at[d - 1],
            device_id={AXIS: me + d},
            device_id_type=pl.DeviceIdType.MESH,
        )

    own_far = ((pos != 3) & (me + 2 < n), (odd == 1) & (me + 3 < n), odd == 0)

    paced = (pos == 2) & (me + 2 < n)

    def send_own(h):
        @pl.when(own_far[0] & ((pos != 2) | (h < AHEAD)))
        def _():
            push(h, own, 2, 0, me + 2).start()

        @pl.when(own_far[1])
        def _():
            push(h, own, 3, 1, me + 3).start()

        @pl.when(own_far[2])
        def _():
            push(h, own, 1, 2, me + 1).start()

    def wait_arrival(h, d):
        push(h, own, d, 0, partner).wait_recv()

    has = tuple(me >= d for d in range(1, PRIOR + 1))
    relays = (pos == 2) & has[2]

    def stage_a(h):
        @pl.when(relays)
        def _():
            wait_arrival(h, 3)
            push(h, slot(3), 2, 1, me - 1).start()

        @pl.when(paced & (h + AHEAD < CHUNKS))
        def _():
            push(h + AHEAD, own, 2, 0, me + 2).start()

    def stage_b(h):
        @pl.when(has[1])
        def _():
            wait_arrival(h, 2)

            @pl.when(odd == 0)
            def _():
                push(h, slot(2), 3, 3, partner).start()

            @pl.when(odd == 1)
            def _():
                push(h, slot(2), 1, 3, partner).start()

    def stage_c(h):
        @pl.when(has[0])
        def _():
            wait_arrival(h, 1)

        @pl.when(has[2] & (pos != 2))
        def _():
            wait_arrival(h, 3)

    local_seg.wait()
    for d in range(1, PRIOR + 1):
        @pl.when(me + d < n)
        def _():
            seg_push(d).start()

    def start_own(h, carry):
        key_copy, value_copy = local_kv(h)
        key_copy.wait()
        send_own(2 * h)
        value_copy.wait()
        send_own(2 * h + 1)
        return carry

    lax.fori_loop(0, KVH, start_own, 0)

    for d in range(1, PRIOR + 1):
        @pl.when(me >= d)
        def _():
            seg_push(d).wait_recv()

    seg_q = jnp.transpose(jnp.broadcast_to(segw[PRIOR], (128, tok)))
    for block in range((PRIOR + 1) * tok // 128):
        shard, part = divmod(block * 128, tok)
        seg_k = jnp.broadcast_to(segw[shard][:, part:part + 128], (tok, 128))
        key_idx = lax.broadcasted_iota(jnp.int32, (tok, 128), 1) + block * 128
        query_idx = lax.broadcasted_iota(jnp.int32, (tok, 128), 0) + PRIOR * tok
        allowed = (seg_k == seg_q) & (key_idx <= query_idx)
        bias[:, block * 128:(block + 1) * 128] = jnp.where(allowed, 0.0, LOW)

    half = tok // 2
    span = PRIOR * tok + half

    def score(g, rb, j0):
        rows, keys = pl.ds(rb * half, half), pl.ds(rb * half, span)
        q = jnp.concatenate([qv[rows, pl.ds(pl.multiple_of((g * GROUP + j) * HD, HD), HD)] for j in range(j0, j0 + BATCH)], axis=0)
        return lax.dot_general(q, kv[2 * g, keys, :], (((1,), (1,)), ((), ())), preferred_element_type=jnp.float32)

    def soften(s, rb):
        s = s.reshape(BATCH, half, span) + bias[pl.ds(rb * half, half), pl.ds(rb * half, span)][None]
        top = jnp.max(s, axis=-1, keepdims=True)
        return jnp.exp2((s - top) * SCALE).astype(jnp.bfloat16).reshape(BATCH * half, span)

    def gather(g, p, rb):
        ones = jnp.ones((span, HD), jnp.bfloat16)
        wide = jnp.concatenate([kv[2 * g + 1, pl.ds(rb * half, span), :], ones], axis=1)
        o = jnp.dot(p, wide, preferred_element_type=jnp.float32)
        o = (o[:, :HD] / o[:, HD:]).astype(jnp.bfloat16).astype(jnp.float32) * (1.0 / math.sqrt(HEADS))
        return [o[j * half:(j + 1) * half] for j in range(BATCH)]

    def attend_group(g):
        for rb in range(2):
            mixed = butterfly(gather(g, soften(score(g, rb, 0), rb), rb))
            for j in range(GROUP):
                acc[g, j, pl.ds(rb * half, half), :] = mixed[j]

    early = pos != 1

    def relay(c):
        @pl.when(early & (c < CHUNKS))
        def _():
            stage_a(c)
            stage_b(c)

    relay(0)
    relay(1)

    def step(g, carry):
        relay(2 * g + 2)
        relay(2 * g + 3)

        @pl.when(pos == 1)
        def _():
            stage_b(2 * g)
            stage_b(2 * g + 1)

        stage_c(2 * g)
        stage_c(2 * g + 1)
        local_q(g).wait()
        attend_group(g)
        return carry

    lax.fori_loop(0, KVH, step, 0)

    def drain(flow):
        pltpu.make_async_remote_copy(
            src_ref=kv.at[:, own, :],
            dst_ref=kv.at[:, own, :],
            send_sem=send_sem.at[flow],
            recv_sem=recv_sem.at[0, 0],
            device_id={AXIS: partner},
            device_id_type=pl.DeviceIdType.MESH,
        ).wait_send()

    for flow, when in enumerate((own_far[0], own_far[1] | relays, own_far[2], has[1])):
        @pl.when(when)
        def _():
            drain(flow)

    for d in range(1, PRIOR + 1):
        @pl.when(me + d < n)
        def _():
            seg_push(d).wait_send()


def mix_kernel(rows, acc, out, held, sem):
    count = out.shape[0] // rows

    def leave(i):
        part = pl.ds(pl.multiple_of(i * rows, rows), rows)
        return pltpu.make_async_copy(held.at[part], out.at[part], sem.at[i])

    def body(i, carry):
        part = pl.ds(pl.multiple_of(i * rows, rows), rows)
        for j in range(GROUP):
            mixed = butterfly([acc[g, j, part, :] for g in range(KVH)])
            for g in range(KVH):
                col = (g * GROUP + j) * HD
                held[part, col:col + HD] = mixed[g].astype(jnp.bfloat16)
        leave(i).start()
        return carry

    def finish(i, carry):
        leave(i).wait()
        return carry

    lax.fori_loop(0, count, body, 0)
    lax.fori_loop(0, count, finish, 0)


def per_device(n, queries, keys, values, segments):
    tok = queries.shape[0]
    hbm = pl.BlockSpec(memory_space=pl.ANY)
    vmem = pl.BlockSpec(memory_space=pltpu.VMEM)
    acc = pl.pallas_call(
        functools.partial(attend_kernel, n, tok),
        out_shape=pltpu.VMEM((KVH, GROUP, tok, HD), jnp.float32),
        in_specs=[hbm] * 4,
        out_specs=vmem,
        scratch_shapes=[
            pltpu.VMEM((tok, HEADS * HD), jnp.bfloat16),
            pltpu.VMEM((CHUNKS, (PRIOR + 1) * tok, HD), jnp.bfloat16),
            pltpu.VMEM((PRIOR + 1, 1, tok), jnp.int32),
            pltpu.VMEM((tok, (PRIOR + 1) * tok), jnp.float32),
            pltpu.SemaphoreType.DMA((KVH,)),
            pltpu.SemaphoreType.DMA((CHUNKS,)),
            pltpu.SemaphoreType.DMA,
            pltpu.SemaphoreType.DMA((4,)),
            pltpu.SemaphoreType.DMA((PRIOR, CHUNKS)),
            pltpu.SemaphoreType.DMA((PRIOR,)),
            pltpu.SemaphoreType.DMA((PRIOR,)),
        ],
        compiler_params=pltpu.CompilerParams(
            collective_id=0, has_side_effects=True, vmem_limit_bytes=50 * 2**20
        ),
        name="attend",
    )(queries, keys, values, segments.reshape(1, tok))
    rows = 16
    return pl.pallas_call(
        functools.partial(mix_kernel, rows),
        out_shape=jax.ShapeDtypeStruct((tok, HEADS * HD), jnp.bfloat16),
        in_specs=[vmem],
        out_specs=hbm,
        scratch_shapes=[
            pltpu.VMEM((tok, HEADS * HD), jnp.bfloat16),
            pltpu.SemaphoreType.DMA((tok // rows,)),
        ],
        compiler_params=pltpu.CompilerParams(vmem_limit_bytes=16 * 2**20),
        name="mix",
    )(acc)


def solution(mesh):
    spec = P(("groups", AXIS), None)
    return jax.shard_map(
        functools.partial(per_device, mesh.shape[AXIS]),
        mesh=mesh,
        in_specs=(spec, spec, spec, P(("groups", AXIS))),
        out_specs=spec,
        check_vma=False,
    )
```
